256 devices in a mesh: dp: 16 (over y, x), table: 8 (over z), tensor: 2 (over core).
Axes of the slice: x: 4, y: 4, z: 8, core: 2. Of those that a mesh axis runs over, the one named last changes fastest.
Arguments:
- tokens: bfloat16 [6144, 4096], P('dp', ('table', 'tensor')), may hold values from -6 to 6
- cotangent: bfloat16 [6144, 4096], P('dp', ('table', 'tensor')), may hold values from -6 to 6
- norm_gain: float32 [4096], replicated, may hold values from 0.5 to 2
- gate_weight: bfloat16 [4096, 14336], P('dp', ('table', 'tensor')), may hold values from -0.09375 to 0.09375
- up_weight: bfloat16 [4096, 14336], P('dp', ('table', 'tensor')), may hold values from -0.09375 to 0.09375
- down_weight: bfloat16 [14336, 4096], P(('table', 'tensor'), 'dp'), may hold values from -0.046875 to 0.046875
- table: float32 [16, 65536, 256], P(('table', 'tensor'), 'dp'), may hold values from -4 to 4
- accum: float32 [16, 65536], P(('table', 'tensor'), 'dp'), may hold values from 0.1 to 10
- owner: int32 [16, 6144, 1], P(('table', 'tensor'), 'dp'), may hold values from 0 to 15; in each aligned block of 384 rows (0 to 383, 384 to 767, ..., all dimensions but the last counted through in order) at most 48 rows name the same one
- slot_row: int32 [16, 6144, 1], P(('table', 'tensor'), 'dp'), may hold values from 0 to 4095
Outputs:
- new_table: float32 [16, 65536, 256], P(('table', 'tensor'), 'dp')
- new_accum: float32 [16, 65536], P(('table', 'tensor'), 'dp')
The draws below stay inside these ranges and needn't reach their ends.
Inputs may be any that keep to these rules, and one draw needn't show every extreme that they name: `owner`: read slice by slice, every aligned block of 384 entries (the rows of one device) names no value more than 48 times.
All inputs are finite; a program needn't handle non-finite values.
Results may differ from the reference program's by a relative error of at most 0.009.
Values may be sent and summed in bfloat16 or wider, within the bound.
A program may use at most 128 MiB of HBM per device.

```python
import math
import jax
import jax.numpy as jnp
import numpy as np
from jax import lax

D = 4096
FF = 14336
SLICE = 256
SLICES = 16
HID_DEV = 896
TOK_DEV = 384
TOKENS = 6144
ROWS_DEV = 4096
ROWS = 65536
CAP = 48
N_DP = 16


def place_ends(values, key, least, top_value):
    extent = values.shape
    spot = [jax.random.randint(jax.random.fold_in(key, axis), (), 0, extent[axis]) for axis in range(len(extent))]
    values = values.at[tuple(spot)].set(least)
    longest = extent.index(max(extent))
    spot[longest] = (spot[longest] + 1) % extent[longest]
    return values.at[tuple(spot)].set(top_value)


def block_levels(key, dims, pieces, low, top_value):
    def one(position, shards_of):
        draws = jax.random.uniform(jax.random.fold_in(jax.random.fold_in(key, 6), position), (shards_of,), jnp.float32, low / len(pieces), top_value / len(pieces))
        return jnp.repeat(jnp.exp(draws), dims[position] // shards_of).reshape((-1,) + (1,) * (len(dims) - position - 1))

    loudness = one(*pieces[0])
    for cut in pieces[1:]:
        loudness = loudness * one(*cut)
    return loudness


def rank_bounds(number_of, lean):
    weights = [(1 << 20) // math.isqrt(standing ** lean) + 1 for standing in range(1, number_of + 1)]
    deviation = 1 + sum(weights) // (1 << 30)
    return np.cumsum(np.array([max(1, weight // deviation) for weight in weights]))


def ranked_ids(rng, extent, amount, lean):
    table = rank_bounds(amount, lean)
    ticket = jax.random.randint(jax.random.fold_in(rng, 1), extent, 0, int(table[amount - 1]))
    rank = jnp.searchsorted(jnp.asarray(table, jnp.int32), ticket, side="right")
    return jax.random.permutation(jax.random.fold_in(rng, 2), amount)[rank].astype(jnp.int32)


def assign_block(own_key, own, number, rows, count, top, most, lean):
    ranking = jax.random.permutation(own_key, count)
    packed, usual = load_shares(count, rows * top, most, lean, True), load_shares(count, rows * top, most, lean, False)
    places = jnp.arange(count)

    def named(lengths, rotation):
        used = int((lengths > 0).sum())
        fixed = max(1, used // 4)
        moved = fixed + (places - fixed + rotation * (used - fixed)) % max(1, count - fixed)
        return jnp.zeros((count,), jnp.int32).at[ranking[jnp.where(places < fixed, places, moved)]].set(jnp.asarray(lengths, jnp.int32))

    lengths = jnp.where(number % 4 == 0, named(packed, number // 4), named(usual, number - number // 4 - 1))
    mixed = jax.random.permutation(jax.random.fold_in(own, 3), count)
    donor, receiver = mixed[0:count // 2 * 2:2], mixed[1:count // 2 * 2:2]
    room = jnp.minimum(lengths[donor] - 1, most - lengths[receiver]) // 2
    room = jnp.where((donor == ranking[0]) | (receiver == ranking[0]) | (lengths[receiver] == 0), 0, jnp.maximum(room, 0))
    moved = jax.random.randint(jax.random.fold_in(own, 4), (count // 2,), 0, 1 << 20) % (room + 1)
    lengths = lengths.at[donor].add(-moved).at[receiver].add(moved)
    items = jnp.searchsorted(jnp.cumsum(lengths), jnp.arange(rows * top), side="right").astype(jnp.int32)
    listing = items.reshape(top, rows).T
    listing = listing[jax.random.permutation(jax.random.fold_in(own, 1), rows)]
    rotation = jax.random.randint(jax.random.fold_in(own, 2), (rows, 1), 0, top)
    return jnp.take_along_axis(listing, (jnp.arange(top)[None, :] + rotation) % top, axis=1)


def load_shares(amount, total, bound, slope, full):
    weights = [(1 << 20) // math.isqrt(grade ** slope) + 1 for grade in range(1, amount + 1)]
    largest = bound if full else min(bound, max(-(-total // amount), total * weights[0] // sum(weights)))
    least = 1 if total - largest >= amount - 1 else 0
    counts, spare = [largest] + [least] * (amount - 1), total - largest - least * (amount - 1)
    while spare > 0:
        free = [i for i in range(1, amount) if counts[i] < largest] or [i for i in range(1, amount) if counts[i] < bound]
        pool, remaining = sum([weights[i] for i in free]), spare
        for i in free:
            addition = min(bound - counts[i], max(1, remaining * weights[i] // pool), spare)
            counts[i] = counts[i] + addition
            spare = spare - addition
    return np.array(counts)


def bell_draw(rng, dims, scale, most, pieces=(), kind=jnp.bfloat16):
    drawn = jax.random.normal(rng, dims, jnp.float32) * scale
    if len(pieces) > 0:
        drawn = block_levels(rng, dims, pieces, -0.22, 0.18) * drawn
    return jnp.clip(drawn, min=-most, max=most).astype(kind)


def setup_inputs(seed: int = 0) -> dict:
    splits = jax.random.split(jax.random.key(seed), 11)
    tokens = bell_draw(splits[0], (TOKENS, D), 1.0, 6.0, ((0, 16), (1, 16)))
    cotangent = bell_draw(splits[1], (TOKENS, D), 1.0, 6.0, ((0, 16), (1, 16)))
    norm_gain = jnp.clip(jnp.exp(jax.random.uniform(splits[2], (D,), jnp.float32, math.log(0.5), math.log(2.0))), 0.5, 2.0)
    gate_weight = bell_draw(splits[3], (D, FF), D ** -0.5, 0.09375, ((0, 16), (1, 16)))
    up_weight = bell_draw(splits[4], (D, FF), D ** -0.5, 0.09375, ((0, 16), (1, 16)))
    down_weight = bell_draw(splits[5], (FF, D), FF ** -0.5, 0.046875, ((0, 16), (1, 16)))
    table = bell_draw(splits[6], (SLICES, ROWS, SLICE), 0.5, 4.0, ((0, 16), (1, 16)), jnp.float32)
    accum = jnp.clip(jnp.exp(math.log(10.0) - 4.6051702 * jax.random.uniform(splits[7], (SLICES, ROWS), jnp.float32) ** block_levels(splits[7], (SLICES, ROWS), ((0, 16), (1, 16)), -0.2, 0.2)), 0.1, 10.0)
    owner_keys = jax.random.split(jax.random.fold_in(splits[8], 1), SLICES * TOKENS // TOK_DEV)
    owner_turns = jax.random.permutation(jax.random.fold_in(splits[8], 3), SLICES * TOKENS // TOK_DEV)
    owner = jax.vmap(lambda own, number: assign_block(jax.random.fold_in(splits[8], 2), own, number, TOK_DEV, N_DP, 1, CAP, 2))(owner_keys, owner_turns).reshape((SLICES, TOKENS, 1))
    slot_row = place_ends(ranked_ids(splits[9], (SLICES, TOKENS, 1), ROWS_DEV, 1), jax.random.fold_in(splits[9], 3), 0, ROWS_DEV - 1).astype(jnp.int32)
    return dict(tokens=tokens, cotangent=cotangent, norm_gain=norm_gain, gate_weight=gate_weight, up_weight=up_weight, down_weight=down_weight, table=table, accum=accum, owner=owner, slot_row=slot_row)


NORM_EPS = 1e-05
LEARNING_RATE = 0.1

def reference(tokens, cotangent, norm_gain, gate_weight, up_weight, down_weight, table, accum, owner, slot_row):
    inputs = tokens.astype(jnp.float32)
    inv_rms = lax.rsqrt(lax.optimization_barrier(jnp.mean(inputs * inputs, axis=-1, keepdims=True)) + NORM_EPS)
    normed = inputs * inv_rms
    hidden_in = (normed * norm_gain).astype(jnp.bfloat16)
    blocks = FF // HID_DEV

    def one_block(running, index):
        offset = (index * HID_DEV).astype(jnp.int32)
        gate_cols = lax.dynamic_slice_in_dim(gate_weight, offset, HID_DEV, 1)
        up_cols = lax.dynamic_slice_in_dim(up_weight, offset, HID_DEV, 1)
        down_rows = lax.dynamic_slice_in_dim(down_weight, offset, HID_DEV, 0)
        gate_act = jnp.dot(hidden_in, gate_cols, preferred_element_type=jnp.float32)
        up_act = jnp.dot(hidden_in, up_cols, preferred_element_type=jnp.float32)
        down_grad = lax.dot_general(cotangent, down_rows, (((1,), (1,)), ((), ())), preferred_element_type=jnp.float32)
        sigmoid_gate = jax.nn.sigmoid(gate_act)
        gate_grad = (down_grad * up_act * sigmoid_gate * (1.0 + gate_act * (1.0 - sigmoid_gate))).astype(jnp.bfloat16)
        up_grad = (down_grad * gate_act * sigmoid_gate).astype(jnp.bfloat16)
        partial_sum = lax.dot_general(gate_grad, gate_cols, (((1,), (1,)), ((), ())), preferred_element_type=jnp.float32)
        partial_sum = partial_sum + lax.dot_general(up_grad, up_cols, (((1,), (1,)), ((), ())), preferred_element_type=jnp.float32)
        rounded = lax.optimization_barrier(partial_sum.astype(jnp.bfloat16))
        return (running + rounded.astype(jnp.float32), None)
    start_sum = jnp.zeros(inputs.shape, jnp.float32)
    summed, _ = lax.scan(one_block, start_sum, jnp.arange(blocks, dtype=jnp.int32))
    normed_grad = summed * norm_gain
    row_mean = lax.optimization_barrier(jnp.mean(normed_grad * normed, axis=-1, keepdims=True))
    embed_grad = (cotangent.astype(jnp.float32) + inv_rms * (normed_grad - normed * row_mean)).astype(jnp.bfloat16)
    per_table = jnp.transpose(embed_grad.reshape(TOKENS, SLICES, SLICE), (1, 0, 2)).astype(jnp.float32)
    row_index = (owner[:, :, 0] * ROWS_DEV + slot_row[:, :, 0]).astype(jnp.int32)

    def per_slice(operands):
        weights_in, accum_in, grads_in, index_in = operands
        row_grad = jax.ops.segment_sum(grads_in, index_in, num_segments=ROWS)
        accum_out = accum_in + lax.optimization_barrier(jnp.mean(row_grad * row_grad, axis=-1))
        table_out = weights_in - LEARNING_RATE * row_grad * lax.rsqrt(accum_out)[:, None]
        return (table_out, accum_out)
    new_table, new_accum = lax.map(per_slice, (table, accum, per_table, row_index))
    return (new_table, new_accum)
```

```python
import jax
import jax.numpy as jnp
from jax import lax
from jax.experimental import pallas as pl
from jax.experimental.pallas import tpu as pltpu
from jax.sharding import PartitionSpec as P

NORM_EPS = 1e-05
LEARNING_RATE = 0.1

NB = 7
HB = 128
TOK = 384
FW = 256
NC = 16
UNIT = 384
CAP = 48
NP = 16
SLOTS = NP * CAP
ROWS = 4096
F32 = jnp.float32
BF16 = jnp.bfloat16
MESH = pl.DeviceIdType.MESH
NT = (((1,), (1,)), ((), ()))
ORDER = (4, 3, -3, 2, -2, 1, -1, 0)


def eye():
    return lax.broadcasted_iota(jnp.int32, (128, 128), 0) == lax.broadcasted_iota(
        jnp.int32, (128, 128), 1
    )


def to_row(col):
    return jnp.sum(jnp.where(eye(), col, 0.0), axis=0, keepdims=True)


def to_col(row):
    return jnp.sum(jnp.where(eye(), row, 0.0), axis=1, keepdims=True)


def main_kernel(
    tok_h,
    cot_h,
    gain,
    gate,
    up,
    down,
    owner,
    slot,
    rows_out,
    ids_out,
    w,
    tc,
    hid,
    part,
    inv,
    acc_gu,
    acc_d,
    grads,
    rsum,
    sbs,
    sbr,
    rs_s,
    rs_r,
    rm_s,
    rm_r,
    place,
    ids_s,
    ids_r,
    snd,
    rcv,
    load_sem,
    tload_sem,
    ag_ss,
    ag_rs,
    tk_ss,
    tk_rs,
    ts_ss,
    ts_rs,
    sb_ss,
    sb_rs,
    rg_ss,
    rg_rs,
    rm_ss,
    rm_rs,
    id_ss,
    id_rs,
    rw_ss,
    rw_rs,
):
    dp = lax.axis_index("dp")
    z = lax.axis_index("table")
    c = lax.axis_index("tensor")
    y = lax.div(dp, 4)
    x = lax.rem(dp, 4)
    grp = 2 * z + c

    def m4(v):
        return lax.rem(v + 8, 4)

    def m8(v):
        return lax.rem(v + 16, 8)

    def m16(v):
        return lax.rem(v + 16, 16)

    def remote(src, dst, ss, rs, dev):
        return pltpu.make_async_remote_copy(
            src_ref=src, dst_ref=dst, send_sem=ss, recv_sem=rs, device_id=dev, device_id_type=MESH
        )

    def wload(b):
        cols = pl.ds(b * HB, HB)
        own = w.at[b, y, x]
        return (
            pltpu.make_async_copy(
                gate.at[:, cols], own.at[pl.ds(0, 256), pl.ds(0, HB)], load_sem.at[b, 0]
            ),
            pltpu.make_async_copy(
                up.at[:, cols], own.at[pl.ds(0, 256), pl.ds(HB, HB)], load_sem.at[b, 1]
            ),
            pltpu.make_async_copy(down.at[cols, :], own.at[pl.ds(256, HB), :], load_sem.at[b, 2]),
        )

    tloads = (
        pltpu.make_async_copy(tok_h, tc.at[z, c, pl.ds(0, TOK)], tload_sem.at[0]),
        pltpu.make_async_copy(cot_h, tc.at[z, c, pl.ds(TOK, TOK)], tload_sem.at[1]),
    )
    for copy in wload(0) + tloads:
        copy.start()
    for b in range(1, NB):
        for copy in wload(b):
            copy.start()

    barrier = pltpu.get_barrier_semaphore()
    for k in range(1, 16):
        pl.semaphore_signal(barrier, inc=1, device_id=(m16(dp + k), z, c), device_id_type=MESH)
        peer = m16(grp + k)
        pl.semaphore_signal(
            barrier,
            inc=1,
            device_id=(dp, lax.div(peer, 2), lax.rem(peer, 2)),
            device_id_type=MESH,
        )
    pl.semaphore_wait(barrier, 30)

    def piece(b, p, second, off, rows):
        if p == 0 and not second:
            return w.at[b, y, m4(x + off), rows]
        if p == 0:
            return w.at[b, m4(y + off), :, rows]
        if not second:
            return w.at[b, m4(y + off), x, rows]
        return w.at[b, :, m4(x + off), rows]

    def ag(b, p, s, d, arriving):
        step = 1 if d == 0 else -1
        second = s >= 2
        rows = pl.ds(192 * p, 192) if s % 2 == 0 else pl.ds(192 * p + 96 * d, 96)
        off = -step * (s % 2) - (step if arriving else 0)
        ref = piece(b, p, second, off, rows)
        along_x = (p == 0) != second
        nxt = y * 4 + m4(x + step) if along_x else m4(y + step) * 4 + x
        return remote(ref, ref, ag_ss.at[b, p, s, d], ag_rs.at[b, p, s, d], (nxt, z, c))

    def ag_start(b, s):
        for d in range(2):
            for p in range(2):
                ag(b, p, s, d, False).start()

    def ag_pass(b, s):
        for d in range(2):
            for p in range(2):
                ag(b, p, s, d, True).wait_recv()
                if s % 2 == 0:
                    ag(b, p, s + 1, d, False).start()

    def ag_turn(b):
        ag_pass(b, 1)
        ag_start(b, 2)

    def tk(s, d, arriving):
        step = 1 if d == 0 else -1
        rows = pl.ds(0, 2 * TOK) if s < 3 else pl.ds(TOK * d, TOK)
        ref = tc.at[m8(z - step * (s + (1 if arriving else 0))), c, rows]
        return remote(ref, ref, tk_ss.at[s, d], tk_rs.at[s, d], (dp, m8(z + step), c))

    def tk_sib(m, arriving):
        ref = tc.at[m8(z + ORDER[m]), (1 - c) if arriving else c]
        return remote(ref, ref, ts_ss.at[m], ts_rs.at[m], (dp, z, 1 - c))

    def tk_pass(s):
        for d in range(2):
            tk(s, d, True).wait_recv()
            if s < 3:
                tk(s + 1, d, False).start()
        if s < 3:
            tk_sib(ORDER.index(s + 1), False).start()
            tk_sib(ORDER.index(-s - 1), False).start()
        else:
            tk_sib(0, False).start()

    for copy in tloads:
        copy.wait()
    for d in range(2):
        tk(0, d, False).start()
    for b in range(3):
        for copy in wload(b):
            copy.wait()
        ag_start(b, 0)
    tk_sib(7, False).start()
    ag_pass(0, 0)
    for b in range(3, NB):
        for copy in wload(b):
            copy.wait()
    ag_pass(1, 0)
    ag_turn(0)

    part[...] = jnp.zeros_like(part)
    rsum[...] = jnp.zeros_like(rsum)

    own = owner[...]
    holder = lax.broadcasted_iota(jnp.int32, (NP, TOK), 0)
    marks = jnp.where(holder == own, 1.0, 0.0)
    before = jnp.where(
        lax.broadcasted_iota(jnp.int32, (TOK, TOK), 0)
        <= lax.broadcasted_iota(jnp.int32, (TOK, TOK), 1),
        1.0,
        0.0,
    ).astype(BF16)
    ranks = jnp.dot(marks.astype(BF16), before, preferred_element_type=F32)
    rank = (jnp.sum(ranks * marks, axis=0, keepdims=True) - 1.0).astype(jnp.int32)
    spots = lax.broadcasted_iota(jnp.int32, (SLOTS, TOK), 0)
    place[...] = jnp.where(spots == own * CAP + rank, 1.0, 0.0).astype(BF16)
    lanes = jnp.where(spots == dp * CAP + rank, 1.0, 0.0).astype(BF16)
    named = slot[...] + 1
    high = lax.shift_right_logical(named, 6).astype(F32)
    low = lax.bitwise_and(named, 63).astype(F32)
    high = lax.dot_general((marks * high).astype(BF16), lanes, NT, preferred_element_type=F32)
    low = lax.dot_general((marks * low).astype(BF16), lanes, NT, preferred_element_type=F32)
    ids = high * 64.0 + low
    for k in range(NP):
        ids_s[k] = jnp.broadcast_to(ids[k : k + 1, :], (8, SLOTS))

    def ids_copy(k, arriving):
        peer = m16(dp + k)
        return remote(
            ids_s.at[peer], ids_r.at[k], id_ss.at[k], id_rs.at[k], (peer, z, c)
        )

    for k in range(1, NP):
        ids_copy(k, False).start()

    ag_start(3, 0)
    ag_pass(2, 0)
    tk_pass(0)
    ag_turn(1)
    ag_pass(0, 2)
    tk_pass(1)
    ag_start(4, 0)
    ag_pass(3, 0)
    ag_turn(2)
    tk_pass(2)
    ag_pass(1, 2)
    tk_pass(3)
    for m in (7, 5, 6, 3, 4, 1, 2, 0):
        tk_sib(m, True).wait_recv()

    acc_gu[...] = jnp.zeros_like(acc_gu)

    def squares(k, carry):
        v = tc[lax.div(k, 2), lax.rem(k, 2), pl.ds(0, TOK), :].astype(F32)
        acc_gu[...] += v * v
        return carry

    lax.fori_loop(0, NC, squares, 0)
    inv[...] = lax.rsqrt(jnp.sum(acc_gu[...], axis=1, keepdims=True) * (1.0 / 4096) + NORM_EPS)

    def normalise(k, carry):
        v = tc[lax.div(k, 2), lax.rem(k, 2), pl.ds(0, TOK), :].astype(F32)
        hid[k] = ((v * inv[...]) * gain[pl.ds(k, 1), :]).astype(BF16)
        return carry

    lax.fori_loop(0, NC, normalise, 0)

    def block_grads(b):
        acc_gu[...] = jnp.zeros_like(acc_gu)
        acc_d[...] = jnp.zeros_like(acc_d)

        def four(q, carry):
            gu = jnp.zeros((TOK, FW), F32)
            dg = jnp.zeros((TOK, HB), F32)
            for j in range(4):
                gu += jnp.dot(
                    hid[4 * q + j], w[b, q, j, pl.ds(0, 256), :], preferred_element_type=F32
                )
                dg += lax.dot_general(
                    tc[2 * q + j // 2, j % 2, pl.ds(TOK, TOK), :],
                    w[b, q, j, pl.ds(256, HB), :],
                    NT,
                    preferred_element_type=F32,
                )
            acc_gu[...] += gu
            acc_d[...] += dg
            return carry

        lax.fori_loop(0, 4, four, 0)
        ga = acc_gu[:, pl.ds(0, HB)]
        ua = acc_gu[:, pl.ds(HB, HB)]
        dg = acc_d[...]
        s = 1.0 / (1.0 + jnp.exp(-ga))
        gg = (dg * ua * s * (1.0 + ga * (1.0 - s))).astype(BF16)
        ug = (dg * ga * s).astype(BF16)
        grads[:, pl.ds(0, HB)] = gg
        grads[:, pl.ds(HB, HB)] = ug
        rsum[...] += gg.astype(F32) * ga + ug.astype(F32) * ua

    def back(b, k):
        return lax.dot_general(
            grads[...],
            w[b, lax.div(k, 4), lax.rem(k, 4), pl.ds(0, 256), :],
            NT,
            preferred_element_type=F32,
        )

    def compute(b):
        block_grads(b)

        def chunk(k, carry):
            part[k] += back(b, k)
            return carry

        lax.fori_loop(0, NC, chunk, 0)

    ag_pass(0, 3)
    compute(0)

    def tick(i, carry):
        @pl.when(i + 3 < NB)
        def _():
            ag_start(i + 3, 0)

        @pl.when(i + 2 < NB)
        def _():
            ag_pass(i + 2, 0)

        @pl.when(i + 1 < NB)
        def _():
            ag_turn(i + 1)

        ag_pass(i, 2)
        ag_pass(i - 1, 3)
        compute(i - 1)
        return carry

    lax.fori_loop(2, NB, tick, 0)

    total_ids = ids_s[dp]
    for k in range(1, NP):
        ids_copy(k, True).wait_recv()
        total_ids += ids_r[k]
    ids_out[...] = total_ids.astype(jnp.int32) - 1

    last = NB - 1
    ag_pass(last, 3)
    block_grads(last)

    rm_s[...] = jnp.zeros_like(rm_s)
    for q in range(3):
        col = jnp.sum(rsum[pl.ds(128 * q, 128), :], axis=1, keepdims=True)
        rm_s[pl.ds(q, 1), :] = to_row(col)

    def rm_copy(k):
        peer = m16(grp + k)
        return remote(
            rm_s,
            rm_r.at[k],
            rm_ss.at[k],
            rm_rs.at[k],
            (dp, lax.div(peer, 2), lax.rem(peer, 2)),
        )

    def sib(m):
        return remote(sbs.at[m], sbr.at[m], sb_ss.at[m], sb_rs.at[m], (dp, z, 1 - c))

    def finish(m):
        zz = m8(z + ORDER[m])
        k = 2 * zz + 1 - c
        sbs[m] = (part[k] + back(last, k)).astype(BF16)
        sib(m).start()
        k = 2 * zz + c
        part[k] += back(last, k)

    def mine(m, sub):
        rows = pl.ds(192 * sub, 192)
        k = 2 * m8(z + ORDER[m]) + c
        return part[k, rows, :] + sbr[m, rows, :].astype(F32)

    def ring(d, n):
        step = 1 if d == 0 else -1
        return remote(
            rs_s.at[d, n], rs_r.at[d, n], rg_ss.at[d, n], rg_rs.at[d, n], (dp, m8(z + step), c)
        )

    finish(0)
    finish(1)
    finish(2)
    for k in range(1, NC):
        rm_copy(k).start()
    sib(0).wait_recv()
    for d in range(2):
        rs_s[d, 0] = mine(0, d).astype(BF16)
        ring(d, 0).start()
    sib(1).wait_recv()
    sib(2).wait_recv()
    for d in range(2):
        rs_s[d, 2 - d] = mine(1 + d, 1 - d).astype(BF16)
        ring(d, 2 - d).start()
    for m in range(3, 8):
        finish(m)
    for d in range(2):
        ring(d, 0).wait_recv()
        rs_s[d, 1 + d] = (mine(1 + d, d) + rs_r[d, 0].astype(F32)).astype(BF16)
        ring(d, 1 + d).start()
    for hop in range(2):
        sib(3 + 2 * hop).wait_recv()
        sib(4 + 2 * hop).wait_recv()
        for turn in range(2):
            for d in range(2):
                sub = (1 - d) if turn == 0 else d
                got = 1 + 2 * hop + sub
                ring(d, got).wait_recv()
                rs_s[d, got + 2] = (
                    mine(3 + 2 * hop + d, sub) + rs_r[d, got].astype(F32)
                ).astype(BF16)
                ring(d, got + 2).start()

    rm_total = rm_s[...]
    for k in range(1, NC):
        rm_copy(k).wait_recv()
        rm_total += rm_r[k]
    rm_total = rm_total * (1.0 / 4096)
    means = jnp.concatenate([to_col(rm_total[q : q + 1, :]) for q in range(3)], axis=0)
    sib(7).wait_recv()
    my_gain = gain[pl.ds(grp, 1), :]
    halves = []
    for sub in range(2):
        ring(0, 5 + sub).wait_recv()
        ring(1, 5 + sub).wait_recv()
        rows = pl.ds(192 * sub, 192)
        total = mine(7, sub) + rs_r[0, 5 + sub].astype(F32) + rs_r[1, 5 + sub].astype(F32)
        iv = inv[rows, :]
        normed = tc[z, c, rows, :].astype(F32) * iv
        ct = tc[z, c, pl.ds(TOK + 192 * sub, 192), :].astype(F32)
        mean = means[192 * sub : 192 * sub + 192, :]
        halves.append((ct + iv * (total * my_gain - normed * mean)).astype(BF16))
    embedded = jnp.concatenate(halves, axis=0)

    for k in range(NP):
        snd[k] = jnp.dot(
            place[pl.ds(CAP * k, CAP), :], embedded, preferred_element_type=F32
        ).astype(BF16)

    def row_copy(k):
        peer = m16(dp + k)
        return remote(snd.at[peer], rcv.at[dp], rw_ss.at[k], rw_rs.at[k], (peer, z, c))

    def row_arrival(k):
        src = m16(dp - k)
        return remote(snd.at[src], rcv.at[src], rw_ss.at[k], rw_rs.at[k], (src, z, c))

    for k in range(1, NP):
        row_copy(k).start()
    rcv[dp] = snd[dp]

    def sent(b, carry):
        for p in range(2):
            for s in range(4):
                for d in range(2):
                    ag(b, p, s, d, False).wait_send()
        return carry

    lax.fori_loop(0, NB, sent, 0)
    for s in range(4):
        for d in range(2):
            tk(s, d, False).wait_send()
    for m in range(8):
        tk_sib(m, False).wait_send()
        sib(m).wait_send()
    for d in range(2):
        for n in range(7):
            ring(d, n).wait_send()
    for k in range(1, NP):
        rm_copy(k).wait_send()
        ids_copy(k, False).wait_send()
    for k in range(1, NP):
        row_arrival(k).wait_recv()
    rows_out[...] = rcv[...]
    for k in range(1, NP):
        row_copy(k).wait_send()


def update_kernel(ids, rows, table, accum, table_out, accum_out):
    n = table.shape[1]
    base = pl.program_id(0) * n
    row = lax.broadcasted_iota(jnp.int32, (n, SLOTS), 0) + base
    hot = jnp.where(row == ids[0:1, :], 1.0, 0.0).astype(BF16)
    grad = jnp.dot(hot, rows[...], preferred_element_type=F32)
    square = jnp.sum(grad * grad, axis=1, keepdims=True) * (1.0 / FW)
    for q in range(n // 128):
        part = slice(128 * q, 128 * (q + 1))
        fresh = to_col(accum[0:1, pl.ds(128 * q, 128)]) + square[part, :]
        accum_out[0:1, pl.ds(128 * q, 128)] = to_row(fresh)
        table_out[0, pl.ds(128 * q, 128), :] = table[0, pl.ds(128 * q, 128), :] - (
            LEARNING_RATE * grad[part, :] * lax.rsqrt(fresh)
        )


def shards(
    tokens, cotangent, norm_gain, gate_weight, up_weight, down_weight, table, accum, owner, slot_row
):
    any_space = pl.BlockSpec(memory_space=pl.ANY)
    in_vmem = pl.BlockSpec(memory_space=pltpu.VMEM)
    dma = pltpu.SemaphoreType.DMA
    rows, ids = pl.pallas_call(
        main_kernel,
        out_shape=(
            jax.ShapeDtypeStruct((NP, CAP, FW), BF16),
            jax.ShapeDtypeStruct((8, SLOTS), jnp.int32),
        ),
        in_specs=[
            any_space,
            any_space,
            in_vmem,
            any_space,
            any_space,
            any_space,
            in_vmem,
            in_vmem,
        ],
        out_specs=(in_vmem, in_vmem),
        scratch_shapes=[
            pltpu.VMEM((NB, 4, 4, UNIT, FW), BF16),
            pltpu.VMEM((8, 2, 2 * TOK, FW), BF16),
            pltpu.VMEM((NC, TOK, FW), BF16),
            pltpu.VMEM((NC, TOK, FW), F32),
            pltpu.VMEM((TOK, 1), F32),
            pltpu.VMEM((TOK, FW), F32),
            pltpu.VMEM((TOK, HB), F32),
            pltpu.VMEM((TOK, FW), BF16),
            pltpu.VMEM((TOK, HB), F32),
            pltpu.VMEM((8, TOK, FW), BF16),
            pltpu.VMEM((8, TOK, FW), BF16),
            pltpu.VMEM((2, 7, 192, FW), BF16),
            pltpu.VMEM((2, 7, 192, FW), BF16),
            pltpu.VMEM((8, 128), F32),
            pltpu.VMEM((NC, 8, 128), F32),
            pltpu.VMEM((SLOTS, TOK), BF16),
            pltpu.VMEM((NP, 8, SLOTS), F32),
            pltpu.VMEM((NP, 8, SLOTS), F32),
            pltpu.VMEM((NP, CAP, FW), BF16),
            pltpu.VMEM((NP, CAP, FW), BF16),
            dma((NB, 3)),
            dma((2,)),
            dma((NB, 2, 4, 2)),
            dma((NB, 2, 4, 2)),
            dma((4, 2)),
            dma((4, 2)),
            dma((8,)),
            dma((8,)),
            dma((8,)),
            dma((8,)),
            dma((2, 7)),
            dma((2, 7)),
            dma((NC,)),
            dma((NC,)),
            dma((NP,)),
            dma((NP,)),
            dma((NP,)),
            dma((NP,)),
        ],
        compiler_params=pltpu.CompilerParams(
            collective_id=0, has_side_effects=True, vmem_limit_bytes=60 * 1024 * 1024
        ),
    )(
        tokens,
        cotangent,
        norm_gain.reshape(NC, FW),
        gate_weight,
        up_weight,
        down_weight,
        owner.reshape(1, TOK),
        slot_row.reshape(1, TOK),
    )
    step = 512
    return pl.pallas_call(
        update_kernel,
        out_shape=(
            jax.ShapeDtypeStruct(table.shape, F32),
            jax.ShapeDtypeStruct(accum.shape, F32),
        ),
        grid=(ROWS // step,),
        in_specs=[
            pl.BlockSpec((8, SLOTS), lambda g: (0, 0)),
            pl.BlockSpec((SLOTS, FW), lambda g: (0, 0)),
            pl.BlockSpec((1, step, FW), lambda g: (0, g, 0)),
            pl.BlockSpec((1, step), lambda g: (0, g)),
        ],
        out_specs=(
            pl.BlockSpec((1, step, FW), lambda g: (0, g, 0)),
            pl.BlockSpec((1, step), lambda g: (0, g)),
        ),
        compiler_params=pltpu.CompilerParams(vmem_limit_bytes=32 * 1024 * 1024),
    )(ids, rows.reshape(SLOTS, FW), table, accum)


def solution(mesh):
    in_specs = (
        P("dp", ("table", "tensor")),
        P("dp", ("table", "tensor")),
        P(),
        P("dp", ("table", "tensor")),
        P("dp", ("table", "tensor")),
        P(("table", "tensor"), "dp"),
        P(("table", "tensor"), "dp", None),
        P(("table", "tensor"), "dp"),
        P(("table", "tensor"), "dp", None),
        P(("table", "tensor"), "dp", None),
    )
    out_specs = (P(("table", "tensor"), "dp", None), P(("table", "tensor"), "dp"))
    return jax.shard_map(shards, mesh=mesh, in_specs=in_specs, out_specs=out_specs, check_vma=False)
```

```python
import jax
import jax.numpy as jnp
from jax import lax
from jax.experimental import pallas as pl
from jax.experimental.pallas import tpu as pltpu
from jax.sharding import PartitionSpec as P

NORM_EPS = 1e-05
LEARNING_RATE = 0.1

NB = 7
HB = 128
TOK = 384
FW = 256
NC = 16
UNIT = 384
CAP = 48
NP = 16
SLOTS = NP * CAP
ROWS = 4096
F32 = jnp.float32
BF16 = jnp.bfloat16
MESH = pl.DeviceIdType.MESH
NT = (((1,), (1,)), ((), ()))
ORDER = (4, 3, -3, 2, -2, 1, -1, 0)
HALF = 192
QA = 128
QB = HALF - QA
STAGES = ((0, 1, 2, 3), (4, 5, 6), (7, 8, 9), (10, 11))


def eye():
    return lax.broadcasted_iota(jnp.int32, (128, 128), 0) == lax.broadcasted_iota(
        jnp.int32, (128, 128), 1
    )


def to_row(col):
    return jnp.sum(jnp.where(eye(), col, 0.0), axis=0, keepdims=True)


def to_col(row):
    return jnp.sum(jnp.where(eye(), row, 0.0), axis=1, keepdims=True)


def main_kernel(
    tok_h,
    cot_h,
    gain,
    gate,
    up,
    down,
    owner,
    slot,
    rows_out,
    ids_out,
    w,
    v,
    rla,
    rlb,
    own,
    tc,
    hid,
    part,
    inv,
    acc_gu,
    acc_d,
    grads,
    rsum,
    xs,
    xr,
    rs_s,
    rs_r,
    fin_s,
    fin_r,
    total,
    rm_s,
    rm_r,
    mi_s,
    mi_r,
    place,
    ids_s,
    ids_r,
    snd,
    rcv,
    load_sem,
    tload_sem,
    half_ss,
    half_rs,
    free_sem,
    ag_ss,
    ag_rs,
    sh_ss,
    sh_rs,
    ex_ss,
    ex_rs,
    tk_ss,
    tk_rs,
    xf_ss,
    xf_rs,
    rg_ss,
    rg_rs,
    fn_ss,
    fn_rs,
    rm_ss,
    rm_rs,
    mi_ss,
    mi_rs,
    id_ss,
    id_rs,
    rw_ss,
    rw_rs,
):
    dp = lax.axis_index("dp")
    z = lax.axis_index("table")
    c = lax.axis_index("tensor")
    y = lax.div(dp, 4)
    x = lax.rem(dp, 4)
    h = lax.rem(x, 2)
    mate = y * 4 + x + 1 - 2 * h
    at_home = c == h
    away = c != h
    grp = 2 * z + c

    def m4(n):
        return lax.rem(n + 8, 4)

    def m8(n):
        return lax.rem(n + 16, 8)

    def m16(n):
        return lax.rem(n + 16, 16)

    def remote(src, dst, ss, rs, dev):
        return pltpu.make_async_remote_copy(
            src_ref=src, dst_ref=dst, send_sem=ss, recv_sem=rs, device_id=dev, device_id_type=MESH
        )

    sibling = (dp, z, 1 - c)

    def wload(b, unit):
        cols = pl.ds(b * HB, HB)
        return (
            pltpu.make_async_copy(
                gate.at[:, cols], unit.at[pl.ds(0, 256), pl.ds(0, HB)], load_sem.at[b, 0]
            ),
            pltpu.make_async_copy(
                up.at[:, cols], unit.at[pl.ds(0, 256), pl.ds(HB, HB)], load_sem.at[b, 1]
            ),
            pltpu.make_async_copy(down.at[cols, :], unit.at[pl.ds(256, HB), :], load_sem.at[b, 2]),
        )

    def tloads(buf, first):
        copies = []
        for hf in range(2):
            rows = pl.ds(HALF * hf, HALF)
            copies.append(
                pltpu.make_async_copy(
                    tok_h.at[rows], buf(hf).at[pl.ds(0, HALF)], tload_sem.at[first + 2 * hf]
                )
            )
            copies.append(
                pltpu.make_async_copy(
                    cot_h.at[rows], buf(hf).at[pl.ds(HALF, HALF)], tload_sem.at[first + 2 * hf + 1]
                )
            )
        return copies

    own_loads = tloads(lambda hf: own.at[hf], 0)
    home_loads = tloads(lambda hf: tc.at[hf, z, c], 4)
    for copy in own_loads:
        copy.start()

    @pl.when(at_home)
    def _():
        for copy in home_loads:
            copy.start()
        for b in range(NB):
            for copy in wload(b, w.at[b, y, x]):
                copy.start()

    @pl.when(away)
    def _():
        for b in range(NB):
            for copy in wload(b, v.at[b, y]):
                copy.start()

    barrier = pltpu.get_barrier_semaphore()
    peers = [(m16(dp + k), z, c) for k in range(1, 16)]
    peers += [(dp, m8(z + k), c) for k in range(1, 8)]
    peers += [(mate, m8(z + k), c) for k in range(1, 8)]
    peers += [sibling, (mate, z, 1 - c)]
    for peer in peers:
        pl.semaphore_signal(barrier, inc=1, device_id=peer, device_id_type=MESH)
    pl.semaphore_wait(barrier, len(peers))

    row_a, row_b = HALF * c, HALF * c + QA
    all_a, all_b = pl.ds(row_a, QA), pl.ds(row_b, QB)

    def half_a(d):
        return pl.ds(row_a + QA // 2 * d, QA // 2)

    def half_b(d):
        return pl.ds(row_b + QB // 2 * d, QB // 2)

    def half(b, unit, arriving):
        ref = unit.at[pl.ds(HALF * (c if arriving else 1 - c), HALF)]
        return remote(ref, ref, half_ss.at[b], half_rs.at[b], sibling)

    def half_start(b):
        @pl.when(at_home)
        def _():
            for copy in wload(b, w.at[b, y, x]):
                copy.wait()
            half(b, w.at[b, y, x], False).start()

        @pl.when(away)
        def _():
            for copy in wload(b, v.at[b, y]):
                copy.wait()
            half(b, v.at[b, y], False).start()

    def half_wait(b):
        @pl.when(at_home)
        def _():
            half(b, v.at[b, y], True).wait_recv()
            half(b, w.at[b, y, x], False).wait_send()
            pl.semaphore_signal(free_sem.at[b], inc=1, device_id=sibling, device_id_type=MESH)

        @pl.when(away)
        def _():
            half(b, w.at[b, y, x], True).wait_recv()

    def message(b, n, d):
        t = 1 if d == 0 else -1
        if n == 0:
            return v.at[b, y, all_a], w.at[b, y, x, all_a], w.at[b, y, m4(x - t), all_a], 0
        if n == 1:
            return w.at[b, y, x, half_a(d)], rla.at[b, d], rla.at[b, d], 0
        if n == 2:
            ref = w.at[b, y, x, all_b]
            return ref, ref, w.at[b, m4(y - t), x, all_b], 1
        if n == 3:
            ref = v.at[b, y, all_b]
            return ref, ref, v.at[b, m4(y - t), all_b], 1
        if n == 4:
            return (
                rla.at[b, d],
                w.at[b, y, m4(x - t), half_a(d)],
                w.at[b, y, m4(x - 2 * t), half_a(d)],
                0,
            )
        if n == 5:
            ref = w.at[b, m4(y - t), x, half_b(d)]
            return ref, ref, w.at[b, m4(y - 2 * t), x, half_b(d)], 1
        if n == 6:
            ref = v.at[b, m4(y - t), half_b(d)]
            return ref, ref, v.at[b, m4(y - 2 * t), half_b(d)], 1
        if n == 7:
            ref = w.at[b, y, :, all_a]
            return ref, ref, w.at[b, m4(y - t), :, all_a], 1
        if n == 8:
            return v.at[b, :, all_b], w.at[b, :, x, all_b], w.at[b, :, m4(x - t), all_b], 0
        if n == 9:
            return w.at[b, :, x, half_b(d)], rlb.at[b, d], rlb.at[b, d], 0
        if n == 10:
            ref = w.at[b, m4(y - t), :, half_a(d)]
            return ref, ref, w.at[b, m4(y - 2 * t), :, half_a(d)], 1
        return (
            rlb.at[b, d],
            w.at[b, :, m4(x - t), half_b(d)],
            w.at[b, :, m4(x - 2 * t), half_b(d)],
            0,
        )

    def ag_send(b, n, d):
        t = 1 if d == 0 else -1
        src, dst, _, axis = message(b, n, d)
        nxt = y * 4 + m4(x + t) if axis == 0 else m4(y + t) * 4 + x
        return remote(src, dst, ag_ss.at[b, n, d], ag_rs.at[b, n, d], (nxt, z, c))

    def ag_start(b, stage):
        for n in STAGES[stage]:
            for d in range(2):
                ag_send(b, n, d).start()

    def ag_wait(b, stage):
        for n in STAGES[stage]:
            for d in range(2):
                _, _, ref, _ = message(b, n, d)
                remote(ref, ref, ag_ss.at[b, n, d], ag_rs.at[b, n, d], sibling).wait_recv()

    def share(b, i, arriving):
        side = (1 - c) if arriving else c
        k = (0, 1, -1, 2)[i % 4]
        if i < 4:
            ref = w.at[b, m4(y + k), :, pl.ds(HALF * side, QA)]
        else:
            ref = w.at[b, :, m4(x + k), pl.ds(HALF * side + QA, QB)]
        return remote(ref, ref, sh_ss.at[b, i], sh_rs.at[b, i], sibling)

    def stage_one(b):
        half_wait(b)
        ag_start(b, 0)

    def stage_two(b):
        ag_wait(b, 0)
        ag_start(b, 1)

    def stage_three(b):
        ag_wait(b, 1)
        ag_start(b, 2)

        @pl.when(away)
        def _():
            pl.semaphore_wait(free_sem.at[b], 1)

        share(b, 0, False).start()
        share(b, 4, False).start()

    def stage_four(b):
        ag_wait(b, 2)
        ag_start(b, 3)
        for i in (1, 2, 5, 6):
            share(b, i, False).start()

    def stage_five(b):
        ag_wait(b, 3)
        share(b, 3, False).start()
        share(b, 7, False).start()
        for i in range(8):
            share(b, i, True).wait_recv()

    def ex_mate(hf, arriving_from=None):
        if arriving_from is None:
            dst = tc.at[hf, z, c]
            return remote(own.at[hf], dst, ex_ss.at[hf, 0], ex_rs.at[hf, c], (mate, z, h))
        dst = tc.at[hf, z, arriving_from]
        return remote(dst, dst, ex_ss.at[hf, 0], ex_rs.at[hf, arriving_from], (mate, z, h))

    def ex_sib(hf, arriving):
        dst = tc.at[hf, z, (1 - c) if arriving else c]
        src = dst if arriving else own.at[hf]
        return remote(src, dst, ex_ss.at[hf, 1], ex_rs.at[hf, 2], sibling)

    def ex_start(hf):
        for copy in own_loads[2 * hf : 2 * hf + 2]:
            copy.wait()
        ex_mate(hf).start()

        @pl.when(away)
        def _():
            ex_sib(hf, False).start()

    def ex_wait(hf):
        @pl.when(at_home)
        def _():
            for copy in home_loads[2 * hf : 2 * hf + 2]:
                copy.wait()
            ex_sib(hf, True).wait_recv()

        @pl.when(away)
        def _():
            for e in range(2):
                ex_mate(hf, e).wait_recv()

    def tk(hf, s, d, e, arriving):
        t = 1 if d == 0 else -1
        ref = tc.at[hf, m8(z - t * (s + (1 if arriving else 0))), e]
        return remote(
            ref, ref, tk_ss.at[hf, s, d, e], tk_rs.at[hf, s, d, e], (dp, m8(z + t), c)
        )

    def tk_start(hf):
        ex_wait(hf)
        for e in range(2):
            for d in range(2):
                tk(hf, 0, d, e, False).start()

    def tk_pass(hf, s):
        if s == 3:
            for d in range(2):
                tk(hf, 3, d, d, True).wait_recv()
            return
        for e in range(2):
            for d in range(2):
                tk(hf, s, d, e, True).wait_recv()
                if s < 2 or d == e:
                    tk(hf, s + 1, d, e, False).start()

    half_start(0)
    ex_start(0)
    half_start(1)
    half_start(2)
    stage_one(0)
    tk_start(0)
    stage_one(1)
    stage_one(2)
    for b in range(3, NB):
        half_start(b)
    stage_two(0)
    ex_start(1)
    stage_two(1)
    stage_three(0)

    part[...] = jnp.zeros_like(part)
    rsum[...] = jnp.zeros_like(rsum)

    own_row = owner[...]
    holder = lax.broadcasted_iota(jnp.int32, (NP, TOK), 0)
    marks = jnp.where(holder == own_row, 1.0, 0.0)
    before = jnp.where(
        lax.broadcasted_iota(jnp.int32, (TOK, TOK), 0)
        <= lax.broadcasted_iota(jnp.int32, (TOK, TOK), 1),
        1.0,
        0.0,
    ).astype(BF16)
    ranks = jnp.dot(marks.astype(BF16), before, preferred_element_type=F32)
    rank = (jnp.sum(ranks * marks, axis=0, keepdims=True) - 1.0).astype(jnp.int32)
    spots = lax.broadcasted_iota(jnp.int32, (SLOTS, TOK), 0)
    place[...] = jnp.where(spots == own_row * CAP + rank, 1.0, 0.0).astype(BF16)
    lanes = jnp.where(spots == dp * CAP + rank, 1.0, 0.0).astype(BF16)
    named = slot[...] + 1
    high = lax.shift_right_logical(named, 6).astype(F32)
    low = lax.bitwise_and(named, 63).astype(F32)
    high = lax.dot_general((marks * high).astype(BF16), lanes, NT, preferred_element_type=F32)
    low = lax.dot_general((marks * low).astype(BF16), lanes, NT, preferred_element_type=F32)
    ids = high * 64.0 + low
    for k in range(NP):
        ids_s[k] = jnp.broadcast_to(ids[k : k + 1, :], (8, SLOTS))

    def ids_copy(k):
        peer = m16(dp + k)
        return remote(ids_s.at[peer], ids_r.at[k], id_ss.at[k], id_rs.at[k], (peer, z, c))

    tk_pass(0, 0)
    for k in range(1, NP):
        ids_copy(k).start()

    def gain_row(k):
        return gain[0:1, pl.ds(pl.multiple_of(k * FW, FW), FW)]

    def normalise(hf):
        rows = pl.ds(HALF * hf, HALF)
        acc_gu[...] = jnp.zeros_like(acc_gu)

        def squares(k, carry):
            t = tc[hf, lax.div(k, 2), lax.rem(k, 2), pl.ds(0, HALF), :].astype(F32)
            acc_gu[...] += t * t
            return carry

        lax.fori_loop(0, NC, squares, 0)
        inv[rows, :] = lax.rsqrt(
            jnp.sum(acc_gu[...], axis=1, keepdims=True) * (1.0 / 4096) + NORM_EPS
        )

        def scale(k, carry):
            t = tc[hf, lax.div(k, 2), lax.rem(k, 2), pl.ds(0, HALF), :].astype(F32)
            hid[k, rows, :] = ((t * inv[rows, :]) * gain_row(k)).astype(BF16)
            return carry

        lax.fori_loop(0, NC, scale, 0)

    def block_grads(b, hf):
        rows = pl.ds(HALF * hf, HALF)
        acc_gu[...] = jnp.zeros_like(acc_gu)
        acc_d[...] = jnp.zeros_like(acc_d)

        def four(q, carry):
            gu = jnp.zeros((HALF, FW), F32)
            dg = jnp.zeros((HALF, HB), F32)
            for j in range(4):
                gu += jnp.dot(
                    hid[4 * q + j, rows, :],
                    w[b, q, j, pl.ds(0, 256), :],
                    preferred_element_type=F32,
                )
                dg += lax.dot_general(
                    tc[hf, 2 * q + j // 2, j % 2, pl.ds(HALF, HALF), :],
                    w[b, q, j, pl.ds(256, HB), :],
                    NT,
                    preferred_element_type=F32,
                )
            acc_gu[...] += gu
            acc_d[...] += dg
            return carry

        lax.fori_loop(0, 4, four, 0)
        ga = acc_gu[:, pl.ds(0, HB)]
        ua = acc_gu[:, pl.ds(HB, HB)]
        dg = acc_d[...]
        s = 1.0 / (1.0 + jnp.exp(-ga))
        gg = (dg * ua * s * (1.0 + ga * (1.0 - s))).astype(BF16)
        ug = (dg * ga * s).astype(BF16)
        grads[rows, pl.ds(0, HB)] = gg
        grads[rows, pl.ds(HB, HB)] = ug
        rsum[rows, :] += gg.astype(F32) * ga + ug.astype(F32) * ua

    def back(b, k, rows):
        return lax.dot_general(
            grads[rows, :],
            w[b, lax.div(k, 4), lax.rem(k, 4), pl.ds(0, 256), :],
            NT,
            preferred_element_type=F32,
        )

    def compute(first, end, hf):
        rows = pl.ds(HALF * hf, HALF)

        def one(b, carry):
            block_grads(b, hf)

            def chunk(k, inner):
                part[k, rows, :] += back(b, k, rows)
                return inner

            lax.fori_loop(0, NC, chunk, 0)
            return carry

        lax.fori_loop(first, end, one, 0)

    for i in range(NB):
        if i + 3 < NB:
            stage_one(i + 3)
        if i + 2 < NB:
            stage_two(i + 2)
        if i < 2:
            tk_pass(0, i + 1)
        if i == 1:
            tk_start(1)
        if 2 <= i <= 5:
            tk_pass(1, i - 2)
        if i + 1 < NB:
            stage_three(i + 1)
        stage_four(i)
        if i > 0:
            stage_five(i - 1)
        if i == 1:
            tk_pass(0, 3)
            normalise(0)
            compute(0, 1, 0)
        elif 2 <= i:
            compute(i - 1, i, 0)
        if i == 5:
            normalise(1)
            compute(0, 3, 1)
        if i == 6:
            compute(3, 6, 1)

    total_ids = ids_s[dp]
    for k in range(1, NP):
        ids_copy(k).wait_recv()
        total_ids += ids_r[k]
    ids_out[...] = total_ids.astype(jnp.int32) - 1

    last = NB - 1
    stage_five(last)
    block_grads(last, 0)
    block_grads(last, 1)

    rm_s[...] = jnp.zeros_like(rm_s)
    for q in range(3):
        col = jnp.sum(rsum[pl.ds(128 * q, 128), :], axis=1, keepdims=True)
        rm_s[pl.ds(q, 1), :] = to_row(col)

    def rm_copy(k, far):
        i = k + 8 if far else k
        return remote(
            rm_s,
            rm_r.at[i],
            rm_ss.at[i],
            rm_rs.at[i],
            (mate if far else dp, m8(z + k), c),
        )

    everything = pl.ds(0, TOK)

    def chunk_of(m, kind):
        e = c if kind == 0 else 1 - c
        return 2 * m8(z + ORDER[m]) + e

    def cross(m):
        return remote(xs.at[m], xr.at[m], xf_ss.at[m], xf_rs.at[m], (mate, z, c))

    def finish(m):
        k = chunk_of(m, 1)
        part[k] += back(last, k, everything)

        @pl.when(away)
        def _():
            xs[m] = part[chunk_of(m, 1)].astype(BF16)
            cross(m).start()

        k = chunk_of(m, 0)
        part[k] += back(last, k, everything)

    def mine(kind, m, sub):
        rows = pl.ds(HALF * sub, HALF)
        value = part[chunk_of(m, kind), rows, :]
        if kind == 1:
            value = value + xr[m, rows, :].astype(F32)
        return value

    def ring(kind, d, n):
        t = 1 if d == 0 else -1
        return remote(
            rs_s.at[kind, d, n],
            rs_r.at[kind, d, n],
            rg_ss.at[kind, d, n],
            rg_rs.at[kind, d, n],
            (dp, m8(z + t), c),
        )

    def push(kind, d, n, value):
        rs_s[kind, d, n] = value.astype(BF16)
        ring(kind, d, n).start()

    def got(kind, d, n):
        return rs_r[kind, d, n].astype(F32)

    def hop_one(kind):
        if kind == 1:
            cross(0).wait_recv()
        for d in range(2):
            push(kind, d, 0, mine(kind, 0, d))

    def hop_two(kind, turn):
        for d in range(2):
            if turn == 0:
                if kind == 1:
                    cross(1 + d).wait_recv()
                push(kind, d, 2 - d, mine(kind, 1 + d, 1 - d))
            else:
                ring(kind, d, 0).wait_recv()
                push(kind, d, 1 + d, mine(kind, 1 + d, d) + got(kind, d, 0))

    def hop_later(kind, hop):
        if kind == 1:
            cross(3 + 2 * hop).wait_recv()
            cross(4 + 2 * hop).wait_recv()
        for turn in range(2):
            for d in range(2):
                sub = (1 - d) if turn == 0 else d
                n = 1 + 2 * hop + sub
                ring(kind, d, n).wait_recv()
                push(kind, d, n + 2, mine(kind, 3 + 2 * hop + d, sub) + got(kind, d, n))

    finish(0)
    hop_one(0)
    finish(1)
    finish(2)
    hop_two(0, 0)
    for k in range(1, 8):

        @pl.when(at_home)
        def _():
            rm_copy(k, False).start()

    for k in range(8):

        @pl.when(away)
        def _():
            rm_copy(k, True).start()

    for m in range(3, 8):
        finish(m)
    hop_two(0, 1)

    @pl.when(at_home)
    def _():
        hop_one(1)
        hop_two(1, 0)

    hop_later(0, 0)

    @pl.when(at_home)
    def _():
        hop_two(1, 1)

    hop_later(0, 1)

    @pl.when(at_home)
    def _():
        hop_later(1, 0)
        rm_total = rm_s[...]
        for k in range(1, 8):
            rm_copy(k, False).wait_recv()
            rm_total += rm_r[k]
        for k in range(8):
            rm_copy(k, True).wait_recv()
            rm_total += rm_r[8 + k]
        mi_s[...] = rm_total * (1.0 / 4096)
        for q in range(3):
            mi_s[pl.ds(3 + q, 1), :] = to_row(inv[pl.ds(128 * q, 128), :])

    mi = remote(mi_s, mi_r, mi_ss, mi_rs, sibling)

    def to_mate(sub):
        return remote(
            fin_s.at[sub], fin_r.at[sub], fn_ss.at[sub], fn_rs.at[sub], (mate, z, c)
        )

    def to_sibling(sub):
        return remote(fin_s.at[sub], fin_r.at[sub], fn_ss.at[sub], fn_rs.at[sub], sibling)

    def summed(kind, sub):
        for d in range(2):
            ring(kind, d, 5 + sub).wait_recv()
        return mine(kind, 7, sub) + got(kind, 0, 5 + sub) + got(kind, 1, 5 + sub)

    @pl.when(at_home)
    def _():
        mi.start()
        mi_r[...] = mi_s[...]
        hop_later(1, 1)
        for sub in range(2):
            total[pl.ds(HALF * sub, HALF), :] = summed(0, sub)
        cross(7).wait_recv()
        for sub in range(2):
            fin_s[sub] = summed(1, sub).astype(BF16)
            to_sibling(sub).start()
        for sub in range(2):
            to_mate(sub).wait_recv()
            total[pl.ds(HALF * sub, HALF), :] += fin_r[sub].astype(F32)

    @pl.when(away)
    def _():
        for sub in range(2):
            fin_s[sub] = summed(0, sub).astype(BF16)
            to_mate(sub).start()
        mi.wait_recv()
        for sub in range(2):
            to_sibling(sub).wait_recv()
            total[pl.ds(HALF * sub, HALF), :] = fin_r[sub].astype(F32)

    my_gain = gain_row(grp)
    stats = mi_r[...]
    means = jnp.concatenate([to_col(stats[q : q + 1, :]) for q in range(3)], axis=0)
    scales = jnp.concatenate([to_col(stats[q : q + 1, :]) for q in range(3, 6)], axis=0)
    halves = []
    for sub in range(2):
        part_rows = slice(HALF * sub, HALF * (sub + 1))
        iv = scales[part_rows, :]
        normed = own[sub, pl.ds(0, HALF), :].astype(F32) * iv
        ct = own[sub, pl.ds(HALF, HALF), :].astype(F32)
        grad = total[pl.ds(HALF * sub, HALF), :] * my_gain
        halves.append((ct + iv * (grad - normed * means[part_rows, :])).astype(BF16))
    embedded = jnp.concatenate(halves, axis=0)

    for k in range(NP):
        snd[k] = jnp.dot(
            place[pl.ds(CAP * k, CAP), :], embedded, preferred_element_type=F32
        ).astype(BF16)

    def row_copy(k):
        peer = m16(dp + k)
        return remote(snd.at[peer], rcv.at[dp], rw_ss.at[k], rw_rs.at[k], (peer, z, c))

    def row_arrival(k):
        src = m16(dp - k)
        return remote(snd.at[src], rcv.at[src], rw_ss.at[k], rw_rs.at[k], (src, z, c))

    for k in range(1, NP):
        row_copy(k).start()
    rcv[dp] = snd[dp]

    def sent(b, carry):
        for n in range(12):
            for d in range(2):
                ag_send(b, n, d).wait_send()
        for i in range(8):
            share(b, i, False).wait_send()
        return carry

    lax.fori_loop(0, NB, sent, 0)
    for hf in range(2):
        ex_mate(hf).wait_send()
        for s in range(4):
            for d in range(2):
                for e in range(2):
                    if s < 3 or d == e:
                        tk(hf, s, d, e, False).wait_send()
    for d in range(2):
        for n in range(7):
            ring(0, d, n).wait_send()
    for sub in range(2):
        to_mate(sub).wait_send()
    for k in range(1, NP):
        ids_copy(k).wait_send()

    @pl.when(at_home)
    def _():
        for d in range(2):
            for n in range(7):
                ring(1, d, n).wait_send()
        for k in range(1, 8):
            rm_copy(k, False).wait_send()
        mi.wait_send()

    @pl.when(away)
    def _():
        for m in range(8):
            cross(m).wait_send()
        for k in range(8):
            rm_copy(k, True).wait_send()
        for hf in range(2):
            ex_sib(hf, False).wait_send()
        for b in range(NB):
            half(b, v.at[b, y], False).wait_send()

    for k in range(1, NP):
        row_arrival(k).wait_recv()
    rows_out[...] = rcv[...]
    for k in range(1, NP):
        row_copy(k).wait_send()


def update_kernel(ids, rows, table, accum, table_out, accum_out):
    n = table.shape[1]
    base = pl.program_id(0) * n
    row = lax.broadcasted_iota(jnp.int32, (n, SLOTS), 0) + base
    hot = jnp.where(row == ids[0:1, :], 1.0, 0.0).astype(BF16)
    grad = jnp.dot(hot, rows[...], preferred_element_type=F32)
    square = jnp.sum(grad * grad, axis=1, keepdims=True) * (1.0 / FW)
    for q in range(n // 128):
        part = slice(128 * q, 128 * (q + 1))
        fresh = to_col(accum[0:1, pl.ds(128 * q, 128)]) + square[part, :]
        accum_out[0:1, pl.ds(128 * q, 128)] = to_row(fresh)
        table_out[0, pl.ds(128 * q, 128), :] = table[0, pl.ds(128 * q, 128), :] - (
            LEARNING_RATE * grad[part, :] * lax.rsqrt(fresh)
        )


def shards(
    tokens, cotangent, norm_gain, gate_weight, up_weight, down_weight, table, accum, owner, slot_row
):
    any_space = pl.BlockSpec(memory_space=pl.ANY)
    in_vmem = pl.BlockSpec(memory_space=pltpu.VMEM)
    dma = pltpu.SemaphoreType.DMA
    rows, ids = pl.pallas_call(
        main_kernel,
        out_shape=(
            jax.ShapeDtypeStruct((NP, CAP, FW), BF16),
            jax.ShapeDtypeStruct((8, SLOTS), jnp.int32),
        ),
        in_specs=[
            any_space,
            any_space,
            in_vmem,
            any_space,
            any_space,
            any_space,
            in_vmem,
            in_vmem,
        ],
        out_specs=(in_vmem, in_vmem),
        scratch_shapes=[
            pltpu.VMEM((NB, 4, 4, UNIT, FW), BF16),
            pltpu.VMEM((NB, 4, UNIT, FW), BF16),
            pltpu.VMEM((NB, 2, QA // 2, FW), BF16),
            pltpu.VMEM((NB, 2, 4, QB // 2, FW), BF16),
            pltpu.VMEM((2, TOK, FW), BF16),
            pltpu.VMEM((2, 8, 2, TOK, FW), BF16),
            pltpu.VMEM((NC, TOK, FW), BF16),
            pltpu.VMEM((NC, TOK, FW), F32),
            pltpu.VMEM((TOK, 1), F32),
            pltpu.VMEM((HALF, FW), F32),
            pltpu.VMEM((HALF, HB), F32),
            pltpu.VMEM((TOK, FW), BF16),
            pltpu.VMEM((TOK, HB), F32),
            pltpu.VMEM((8, TOK, FW), BF16),
            pltpu.VMEM((8, TOK, FW), BF16),
            pltpu.VMEM((2, 2, 7, HALF, FW), BF16),
            pltpu.VMEM((2, 2, 7, HALF, FW), BF16),
            pltpu.VMEM((2, HALF, FW), BF16),
            pltpu.VMEM((2, HALF, FW), BF16),
            pltpu.VMEM((TOK, FW), F32),
            pltpu.VMEM((8, 128), F32),
            pltpu.VMEM((16, 8, 128), F32),
            pltpu.VMEM((8, 128), F32),
            pltpu.VMEM((8, 128), F32),
            pltpu.VMEM((SLOTS, TOK), BF16),
            pltpu.VMEM((NP, 8, SLOTS), F32),
            pltpu.VMEM((NP, 8, SLOTS), F32),
            pltpu.VMEM((NP, CAP, FW), BF16),
            pltpu.VMEM((NP, CAP, FW), BF16),
            dma((NB, 3)),
            dma((8,)),
            dma((NB,)),
            dma((NB,)),
            pltpu.SemaphoreType.REGULAR((NB,)),
            dma((NB, 12, 2)),
            dma((NB, 12, 2)),
            dma((NB, 8)),
            dma((NB, 8)),
            dma((2, 2)),
            dma((2, 3)),
            dma((2, 4, 2, 2)),
            dma((2, 4, 2, 2)),
            dma((8,)),
            dma((8,)),
            dma((2, 2, 7)),
            dma((2, 2, 7)),
            dma((2,)),
            dma((2,)),
            dma((16,)),
            dma((16,)),
            dma(()),
            dma(()),
            dma((NP,)),
            dma((NP,)),
            dma((NP,)),
            dma((NP,)),
        ],
        compiler_params=pltpu.CompilerParams(
            collective_id=0, has_side_effects=True, vmem_limit_bytes=61 * 1024 * 1024
        ),
    )(
        tokens,
        cotangent,
        norm_gain.reshape(1, NC * FW),
        gate_weight,
        up_weight,
        down_weight,
        owner.reshape(1, TOK),
        slot_row.reshape(1, TOK),
    )
    step = 512
    return pl.pallas_call(
        update_kernel,
        out_shape=(
            jax.ShapeDtypeStruct(table.shape, F32),
            jax.ShapeDtypeStruct(accum.shape, F32),
        ),
        grid=(ROWS // step,),
        in_specs=[
            pl.BlockSpec((8, SLOTS), lambda g: (0, 0)),
            pl.BlockSpec((SLOTS, FW), lambda g: (0, 0)),
            pl.BlockSpec((1, step, FW), lambda g: (0, g, 0)),
            pl.BlockSpec((1, step), lambda g: (0, g)),
        ],
        out_specs=(
            pl.BlockSpec((1, step, FW), lambda g: (0, g, 0)),
            pl.BlockSpec((1, step), lambda g: (0, g)),
        ),
        compiler_params=pltpu.CompilerParams(vmem_limit_bytes=60 * 1024 * 1024),
    )(ids, rows.reshape(SLOTS, FW), table, accum)


def solution(mesh):
    in_specs = (
        P("dp", ("table", "tensor")),
        P("dp", ("table", "tensor")),
        P(),
        P("dp", ("table", "tensor")),
        P("dp", ("table", "tensor")),
        P(("table", "tensor"), "dp"),
        P(("table", "tensor"), "dp", None),
        P(("table", "tensor"), "dp"),
        P(("table", "tensor"), "dp", None),
        P(("table", "tensor"), "dp", None),
    )
    out_specs = (P(("table", "tensor"), "dp", None), P(("table", "tensor"), "dp"))
    return jax.shard_map(shards, mesh=mesh, in_specs=in_specs, out_specs=out_specs, check_vma=False)
```

```python
import jax
import jax.numpy as jnp
from jax import lax
from jax.experimental import pallas as pl
from jax.experimental.pallas import tpu as pltpu
from jax.sharding import PartitionSpec as P

NORM_EPS = 1e-05
LEARNING_RATE = 0.1

NB = 7
HB = 128
TOK = 384
FW = 256
NC = 16
UNIT = 384
CAP = 48
NP = 16
SLOTS = NP * CAP
ROWS = 4096
STEP = 1024
F32 = jnp.float32
BF16 = jnp.bfloat16
MESH = pl.DeviceIdType.MESH
NT = (((1,), (1,)), ((), ()))
ORDER = (4, 3, -3, 2, -2, 1, -1, 0)
HALF = 192
QA = 128
QB = HALF - QA
STAGES = ((0, 1, 2, 3), (4, 5, 6), (7, 8, 9), (10, 11))
STAGE_OF = (0, 0, 0, 0, 1, 1, 1, 2, 2, 2, 3, 3)
STAGE_ROWS = (
    (2, QA + QA // 2 + 2 * QB),
    (2, QA // 2 + QB),
    (8, QA + QB + QB // 2),
    (8, QA // 2 + QB // 2),
)


def eye():
    return lax.broadcasted_iota(jnp.int32, (128, 128), 0) == lax.broadcasted_iota(
        jnp.int32, (128, 128), 1
    )


def to_row(col):
    return jnp.sum(jnp.where(eye(), col, 0.0), axis=0, keepdims=True)


def to_col(row):
    return jnp.sum(jnp.where(eye(), row, 0.0), axis=1, keepdims=True)


def main_kernel(
    tok_h,
    cot_h,
    gain_h,
    gate,
    up,
    down,
    owner_h,
    slot_h,
    rows_out,
    ids_out,
    gain,
    owner,
    slot,
    ids_v,
    w,
    v,
    rla,
    rlb,
    own,
    tc,
    hid,
    part,
    inv,
    grads,
    rsum,
    xs,
    xr,
    rs_s,
    rs_r,
    fin_s,
    fin_r,
    total,
    rm_s,
    rm_r,
    mi_s,
    mi_r,
    place,
    ids_s,
    ids_r,
    snd,
    small_sem,
    load_sem,
    tload_sem,
    half_ss,
    half_rs,
    free_sem,
    ag_ss,
    ag_rs,
    sh_ss,
    sh_rs,
    ex_ss,
    ex_rs,
    tk_ss,
    tk_rs,
    xf_ss,
    xf_rs,
    rg_ss,
    rg_rs,
    fn_ss,
    fn_rs,
    rm_ss,
    rm_rs,
    mi_ss,
    mi_rs,
    id_ss,
    id_rs,
    rw_ss,
    rw_rs,
):
    dp = lax.axis_index("dp")
    z = lax.axis_index("table")
    c = lax.axis_index("tensor")
    y = lax.div(dp, 4)
    x = lax.rem(dp, 4)
    h = lax.rem(x, 2)
    mate = y * 4 + x + 1 - 2 * h
    at_home = c == h
    away = c != h
    grp = 2 * z + c

    def m4(n):
        return lax.rem(n + 8, 4)

    def m8(n):
        return lax.rem(n + 16, 8)

    def m16(n):
        return lax.rem(n + 16, 16)

    def remote(src, dst, ss, rs, dev):
        return pltpu.make_async_remote_copy(
            src_ref=src, dst_ref=dst, send_sem=ss, recv_sem=rs, device_id=dev, device_id_type=MESH
        )

    sibling = (dp, z, 1 - c)

    barrier = pltpu.get_barrier_semaphore()
    peers = [(m16(dp + k), z, c) for k in range(1, 16)]
    peers += [(dp, m8(z + k), c) for k in range(1, 8)]
    peers += [(mate, m8(z + k), c) for k in range(1, 8)]
    peers += [sibling, (mate, z, 1 - c)]
    for peer in peers:
        pl.semaphore_signal(barrier, inc=1, device_id=peer, device_id_type=MESH)

    def wload(b, unit):
        cols = pl.ds(b * HB, HB)
        return (
            pltpu.make_async_copy(
                gate.at[:, cols], unit.at[pl.ds(0, 256), pl.ds(0, HB)], load_sem.at[b]
            ),
            pltpu.make_async_copy(
                up.at[:, cols], unit.at[pl.ds(0, 256), pl.ds(HB, HB)], load_sem.at[b]
            ),
            pltpu.make_async_copy(down.at[cols, :], unit.at[pl.ds(256, HB), :], load_sem.at[b]),
        )

    def tloads(buf, first):
        copies = []
        for hf in range(2):
            rows = pl.ds(HALF * hf, HALF)
            copies.append(
                pltpu.make_async_copy(
                    tok_h.at[rows], buf(hf).at[pl.ds(0, HALF)], tload_sem.at[first + 2 * hf]
                )
            )
            copies.append(
                pltpu.make_async_copy(
                    cot_h.at[rows], buf(hf).at[pl.ds(HALF, HALF)], tload_sem.at[first + 2 * hf + 1]
                )
            )
        return copies

    own_loads = tloads(lambda hf: own.at[hf], 0)
    home_loads = tloads(lambda hf: tc.at[hf, z, c], 4)
    for copy in own_loads:
        copy.start()
    smalls = [
        pltpu.make_async_copy(src, dst, small_sem.at[i])
        for i, (src, dst) in enumerate(((gain_h, gain), (owner_h, owner), (slot_h, slot)))
    ]
    for copy in smalls:
        copy.start()

    @pl.when(at_home)
    def _():
        for copy in home_loads:
            copy.start()
        for b in range(NB):
            for copy in wload(b, w.at[b, y, x]):
                copy.start()

    @pl.when(away)
    def _():
        for b in range(NB):
            for copy in wload(b, v.at[b, y]):
                copy.start()

    pl.semaphore_wait(barrier, len(peers))

    row_a, row_b = HALF * c, HALF * c + QA
    all_a, all_b = pl.ds(row_a, QA), pl.ds(row_b, QB)

    def half_a(d):
        return pl.ds(row_a + QA // 2 * d, QA // 2)

    def half_b(d):
        return pl.ds(row_b + QB // 2 * d, QB // 2)

    def half(b, unit, arriving):
        ref = unit.at[pl.ds(HALF * (c if arriving else 1 - c), HALF)]
        return remote(ref, ref, half_ss.at[b], half_rs.at[b], sibling)

    def half_start(b):
        @pl.when(at_home)
        def _():
            pltpu.make_async_copy(w.at[b, y, x], w.at[b, y, x], load_sem.at[b]).wait()
            half(b, w.at[b, y, x], False).start()

        @pl.when(away)
        def _():
            pltpu.make_async_copy(v.at[b, y], v.at[b, y], load_sem.at[b]).wait()
            half(b, v.at[b, y], False).start()

    def half_wait(b):
        @pl.when(at_home)
        def _():
            half(b, v.at[b, y], True).wait_recv()
            half(b, w.at[b, y, x], False).wait_send()
            pl.semaphore_signal(free_sem.at[b], inc=1, device_id=sibling, device_id_type=MESH)

        @pl.when(away)
        def _():
            half(b, w.at[b, y, x], True).wait_recv()

    def message(b, n, d):
        t = 1 if d == 0 else -1
        if n == 0:
            return v.at[b, y, all_a], w.at[b, y, x, all_a], 0
        if n == 1:
            return w.at[b, y, x, half_a(d)], rla.at[b, d], 0
        if n == 2:
            ref = w.at[b, y, x, all_b]
            return ref, ref, 1
        if n == 3:
            ref = v.at[b, y, all_b]
            return ref, ref, 1
        if n == 4:
            return rla.at[b, d], w.at[b, y, m4(x - t), half_a(d)], 0
        if n == 5:
            ref = w.at[b, m4(y - t), x, half_b(d)]
            return ref, ref, 1
        if n == 6:
            ref = v.at[b, m4(y - t), half_b(d)]
            return ref, ref, 1
        if n == 7:
            ref = w.at[b, y, :, all_a]
            return ref, ref, 1
        if n == 8:
            return v.at[b, :, all_b], w.at[b, :, x, all_b], 0
        if n == 9:
            return w.at[b, :, x, half_b(d)], rlb.at[b, d], 0
        if n == 10:
            ref = w.at[b, m4(y - t), :, half_a(d)]
            return ref, ref, 1
        return rlb.at[b, d], w.at[b, :, m4(x - t), half_b(d)], 0

    def ag_send(b, n, d):
        t = 1 if d == 0 else -1
        src, dst, axis = message(b, n, d)
        nxt = y * 4 + m4(x + t) if axis == 0 else m4(y + t) * 4 + x
        return remote(src, dst, ag_ss.at[b], ag_rs.at[b, STAGE_OF[n]], (nxt, z, c))

    def ag_start(b, stage):
        for n in STAGES[stage]:
            for d in range(2):
                ag_send(b, n, d).start()

    def ag_wait(b, stage):
        deep, rows = STAGE_ROWS[stage]
        ref = hid.at[pl.ds(0, deep), pl.ds(0, rows)]
        remote(ref, ref, ag_ss.at[b], ag_rs.at[b, stage], sibling).wait_recv()

    def share(b, i):
        side = c
        k = (0, 1, -1, 2)[i % 4]
        if i < 4:
            ref = w.at[b, m4(y + k), :, pl.ds(HALF * side, QA)]
        else:
            ref = w.at[b, :, m4(x + k), pl.ds(HALF * side + QA, QB)]
        return remote(ref, ref, sh_ss.at[b], sh_rs.at[b], sibling)

    def stage_one(b):
        half_wait(b)
        ag_start(b, 0)

    def stage_two(b):
        ag_wait(b, 0)
        ag_start(b, 1)

    def stage_three(b):
        ag_wait(b, 1)
        ag_start(b, 2)

        @pl.when(away)
        def _():
            pl.semaphore_wait(free_sem.at[b], 1)

        share(b, 0).start()
        share(b, 4).start()

    def stage_four(b):
        ag_wait(b, 2)
        ag_start(b, 3)
        for i in (1, 2, 5, 6):
            share(b, i).start()

    def shared(b):
        ref = w.at[b, :, :, pl.ds(0, HALF)]
        return remote(ref, ref, sh_ss.at[b], sh_rs.at[b], sibling)

    def stage_five(b):
        ag_wait(b, 3)
        share(b, 3).start()
        share(b, 7).start()
        shared(b).wait_recv()

    def ex_mate(hf, arriving_from=None):
        if arriving_from is None:
            dst = tc.at[hf, z, c]
            return remote(own.at[hf], dst, ex_ss.at[hf, 0], ex_rs.at[hf, c], (mate, z, h))
        dst = tc.at[hf, z, arriving_from]
        return remote(dst, dst, ex_ss.at[hf, 0], ex_rs.at[hf, arriving_from], (mate, z, h))

    def ex_sib(hf, arriving):
        dst = tc.at[hf, z, (1 - c) if arriving else c]
        src = dst if arriving else own.at[hf]
        return remote(src, dst, ex_ss.at[hf, 1], ex_rs.at[hf, 2], sibling)

    def ex_start(hf):
        for copy in own_loads[2 * hf : 2 * hf + 2]:
            copy.wait()

        @pl.when(away)
        def _():
            ex_sib(hf, False).start()

    def ex_wait(hf):
        @pl.when(at_home)
        def _():
            for copy in home_loads[2 * hf : 2 * hf + 2]:
                copy.wait()
            ex_sib(hf, True).wait_recv()

        @pl.when(away)
        def _():
            for e in range(2):
                ex_mate(hf, e).wait_recv()

    def tk(hf, s, d, e):
        t = 1 if d == 0 else -1
        ref = tc.at[hf, m8(z - t * s), e]
        return remote(ref, ref, tk_ss.at[hf], tk_rs.at[hf, s, e], (dp, m8(z + t), c))

    def tk_wait(hf, s, e):
        ref = hid.at[pl.ds(0, 2 if s < 3 else 1)]
        remote(ref, ref, tk_ss.at[hf], tk_rs.at[hf, s, e], sibling).wait_recv()

    def tk_start(hf):
        ex_wait(hf)
        for e in range(2):
            for d in range(2):
                tk(hf, 0, d, e).start()

    def tk_pass(hf, s):
        for e in range(2):
            tk_wait(hf, s, e)
            for d in range(2):
                if s < 2 or (s == 2 and d == e):
                    tk(hf, s + 1, d, e).start()

    for b in range(3):
        half_start(b)
    ex_start(0)
    stage_one(0)
    stage_one(1)

    @pl.when(at_home)
    def _():
        tk_start(0)

    for b in range(3, NB):
        half_start(b)
    stage_two(0)
    ex_mate(0).start()
    stage_one(2)
    stage_two(1)
    stage_three(0)
    stage_one(3)
    ex_start(1)
    ex_mate(1).start()

    @pl.when(away)
    def _():
        tk_start(0)

    stage_two(2)
    stage_three(1)
    stage_one(4)

    part[...] = jnp.zeros_like(part)
    rsum[...] = jnp.zeros_like(rsum)

    for copy in smalls:
        copy.wait()

    own_row = owner[...]
    holder = lax.broadcasted_iota(jnp.int32, (NP, TOK), 0)
    marks = jnp.where(holder == own_row, 1.0, 0.0)
    before = jnp.where(
        lax.broadcasted_iota(jnp.int32, (TOK, TOK), 0)
        <= lax.broadcasted_iota(jnp.int32, (TOK, TOK), 1),
        1.0,
        0.0,
    ).astype(BF16)
    ranks = jnp.dot(marks.astype(BF16), before, preferred_element_type=F32)
    rank = (jnp.sum(ranks * marks, axis=0, keepdims=True) - 1.0).astype(jnp.int32)
    spots = lax.broadcasted_iota(jnp.int32, (SLOTS, TOK), 0)
    place[...] = jnp.where(spots == own_row * CAP + rank, 1.0, 0.0).astype(BF16)
    lanes = jnp.where(spots == dp * CAP + rank, 1.0, 0.0).astype(BF16)
    named = slot[...] + 1
    high = lax.shift_right_logical(named, 6).astype(F32)
    low = lax.bitwise_and(named, 63).astype(F32)
    high = lax.dot_general((marks * high).astype(BF16), lanes, NT, preferred_element_type=F32)
    low = lax.dot_general((marks * low).astype(BF16), lanes, NT, preferred_element_type=F32)
    ids = high * 64.0 + low
    for k in range(NP):
        ids_s[k] = jnp.broadcast_to(ids[k : k + 1, :], (8, SLOTS))

    def ids_copy(k):
        peer = m16(dp + k)
        return remote(ids_s.at[peer], ids_r.at[k], id_ss, id_rs, (peer, z, c))

    for k in range(1, NP):
        ids_copy(k).start()

    def gain_row(k):
        return gain[0:1, pl.ds(pl.multiple_of(k * FW, FW), FW)]

    def normalise(hf):
        rows = pl.ds(HALF * hf, HALF)
        squares = jnp.zeros((HALF, FW), F32)
        for k in range(NC):
            t = tc[hf, k // 2, k % 2, pl.ds(0, HALF), :].astype(F32)
            squares += t * t
        iv = lax.rsqrt(jnp.sum(squares, axis=1, keepdims=True) * (1.0 / 4096) + NORM_EPS)
        inv[rows, :] = iv
        for k in range(NC):
            t = tc[hf, k // 2, k % 2, pl.ds(0, HALF), :].astype(F32)
            hid[k, rows, :] = ((t * iv) * gain[0:1, pl.ds(k * FW, FW)]).astype(BF16)

    def block_grads(b, *halves):
        n = HALF * len(halves)
        rows = pl.ds(HALF * halves[0], n)
        gu = jnp.zeros((n, FW), F32)
        dgs = [jnp.zeros((HALF, HB), F32) for _ in halves]
        for k in range(NC):
            gu += jnp.dot(
                hid[k, rows, :], w[b, k // 4, k % 4, pl.ds(0, 256), :], preferred_element_type=F32
            )
            for i, hf in enumerate(halves):
                dgs[i] += lax.dot_general(
                    tc[hf, k // 2, k % 2, pl.ds(HALF, HALF), :],
                    w[b, k // 4, k % 4, pl.ds(256, HB), :],
                    NT,
                    preferred_element_type=F32,
                )
        dg = jnp.concatenate(dgs, axis=0)
        ga = gu[:, :HB]
        ua = gu[:, HB:]
        s = 1.0 / (1.0 + jnp.exp(-ga))
        gg = (dg * ua * s * (1.0 + ga * (1.0 - s))).astype(BF16)
        ug = (dg * ga * s).astype(BF16)
        grads[rows, pl.ds(0, HB)] = gg
        grads[rows, pl.ds(HB, HB)] = ug
        rsum[rows, :] += gg.astype(F32) * ga + ug.astype(F32) * ua

    def back(b, rows):
        for k in range(NC):
            part[k, rows, :] += lax.dot_general(
                grads[rows, :],
                w[b, k // 4, k % 4, pl.ds(0, 256), :],
                NT,
                preferred_element_type=F32,
            )

    def compute(first, end, *halves):
        def one(b, carry):
            block_grads(b, *halves)
            back(b, pl.ds(HALF * halves[0], HALF * len(halves)))
            return carry

        if end - first == 1:
            one(first, 0)
        else:
            lax.fori_loop(first, end, one, 0)

    tk_pass(0, 0)
    stage_four(0)
    stage_two(3)
    stage_three(2)
    stage_one(5)
    tk_pass(0, 1)
    stage_four(1)
    stage_two(4)
    stage_three(3)
    stage_one(6)
    tk_pass(0, 2)
    tk_start(1)
    stage_four(2)
    stage_two(5)
    tk_pass(0, 3)
    stage_three(4)
    stage_five(0)
    normalise(0)
    compute(0, 1, 0)
    stage_four(3)
    tk_pass(1, 0)
    stage_two(6)
    stage_three(5)
    stage_five(1)
    compute(1, 2, 0)
    tk_pass(1, 1)
    stage_four(4)
    stage_five(2)
    compute(2, 3, 0)
    stage_three(6)
    tk_pass(1, 2)
    stage_four(5)
    stage_five(3)
    compute(3, 4, 0)
    tk_pass(1, 3)
    normalise(1)
    compute(0, 2, 1)
    stage_four(6)
    compute(2, 4, 1)
    stage_five(4)
    compute(4, 5, 0, 1)
    stage_five(5)
    compute(5, 6, 0, 1)

    total_ids = ids_s[dp]
    others = pl.ds(1, NP - 1)
    all_ids = remote(ids_s.at[others], ids_r.at[others], id_ss, id_rs, sibling)
    all_ids.wait_recv()
    for k in range(1, NP):
        total_ids += ids_r[k]
    ids_v[...] = total_ids.astype(jnp.int32) - 1
    ids_done = pltpu.make_async_copy(ids_v, ids_out, small_sem.at[3])
    ids_done.start()

    last = NB - 1
    stage_five(last)
    block_grads(last, 0, 1)

    rm_s[...] = jnp.zeros_like(rm_s)
    for q in range(3):
        col = jnp.sum(rsum[pl.ds(128 * q, 128), :], axis=1, keepdims=True)
        rm_s[pl.ds(q, 1), :] = to_row(col)

    def rm_copy(k, far):
        i = k + 8 if far else k
        return remote(
            rm_s,
            rm_r.at[i],
            rm_ss,
            rm_rs,
            (mate if far else dp, m8(z + k), c),
        )

    def rm_many(n):
        ref = rm_r.at[pl.ds(1, n)]
        return remote(ref, ref, rm_ss, rm_rs, sibling)

    def chunk_of(m, kind):
        e = c if kind == 0 else 1 - c
        return 2 * m8(z + ORDER[m]) + e

    def cross(m):
        return remote(xs.at[m], xr.at[m], xf_ss, xf_rs.at[m], (mate, z, c))

    def mine(kind, m, sub):
        rows = pl.ds(HALF * sub, HALF)
        value = part[chunk_of(m, kind), rows, :]
        if kind == 1:
            value = value + xr[m, rows, :].astype(F32)
        return value

    def ring(kind, d, n):
        t = 1 if d == 0 else -1
        return remote(
            rs_s.at[kind, d, n],
            rs_r.at[kind, d, n],
            rg_ss.at[kind],
            rg_rs.at[kind, d, n],
            (dp, m8(z + t), c),
        )

    def push(kind, d, n, value):
        rs_s[kind, d, n] = value.astype(BF16)
        ring(kind, d, n).start()

    def got(kind, d, n):
        return rs_r[kind, d, n].astype(F32)

    def hop_one(kind):
        if kind == 1:
            cross(0).wait_recv()
        for d in range(2):
            push(kind, d, 0, mine(kind, 0, d))

    def hop_two(kind, turn):
        for d in range(2):
            if turn == 0:
                if kind == 1:
                    cross(1 + d).wait_recv()
                push(kind, d, 2 - d, mine(kind, 1 + d, 1 - d))
            else:
                ring(kind, d, 0).wait_recv()
                push(kind, d, 1 + d, mine(kind, 1 + d, d) + got(kind, d, 0))

    def hop_later(kind, hop):
        if kind == 1:
            cross(3 + 2 * hop).wait_recv()
            cross(4 + 2 * hop).wait_recv()
        for turn in range(2):
            for d in range(2):
                sub = (1 - d) if turn == 0 else d
                n = 1 + 2 * hop + sub
                ring(kind, d, n).wait_recv()
                push(kind, d, n + 2, mine(kind, 3 + 2 * hop + d, sub) + got(kind, d, n))

    back(last, pl.ds(0, TOK))
    hop_one(0)

    @pl.when(away)
    def _():
        for m in range(8):
            xs[m] = part[chunk_of(m, 1)].astype(BF16)
            cross(m).start()

    hop_two(0, 0)
    for k in range(1, 8):

        @pl.when(at_home)
        def _():
            rm_copy(k, False).start()

    for k in range(8):

        @pl.when(away)
        def _():
            rm_copy(k, True).start()

    hop_two(0, 1)

    @pl.when(at_home)
    def _():
        hop_one(1)
        hop_two(1, 0)

    hop_later(0, 0)

    @pl.when(at_home)
    def _():
        hop_two(1, 1)

    hop_later(0, 1)

    @pl.when(at_home)
    def _():
        hop_later(1, 0)
        rm_total = rm_s[...]
        rm_many(15).wait_recv()
        for k in range(1, 16):
            rm_total += rm_r[k]
        mi_s[...] = rm_total * (1.0 / 4096)
        for q in range(3):
            mi_s[pl.ds(3 + q, 1), :] = to_row(inv[pl.ds(128 * q, 128), :])

    mi = remote(mi_s, mi_r, mi_ss, mi_rs, sibling)

    def to_mate(sub):
        return remote(
            fin_s.at[sub], fin_r.at[sub], fn_ss.at[sub], fn_rs.at[sub], (mate, z, c)
        )

    def to_sibling(sub):
        return remote(fin_s.at[sub], fin_r.at[sub], fn_ss.at[sub], fn_rs.at[sub], sibling)

    def summed(kind, sub):
        for d in range(2):
            ring(kind, d, 5 + sub).wait_recv()
        return mine(kind, 7, sub) + got(kind, 0, 5 + sub) + got(kind, 1, 5 + sub)

    @pl.when(at_home)
    def _():
        mi.start()
        mi_r[...] = mi_s[...]
        hop_later(1, 1)
        for sub in range(2):
            total[pl.ds(HALF * sub, HALF), :] = summed(0, sub)
        cross(7).wait_recv()
        for sub in range(2):
            fin_s[sub] = summed(1, sub).astype(BF16)
            to_sibling(sub).start()
        for sub in range(2):
            to_mate(sub).wait_recv()
            total[pl.ds(HALF * sub, HALF), :] += fin_r[sub].astype(F32)

    @pl.when(away)
    def _():
        for sub in range(2):
            fin_s[sub] = summed(0, sub).astype(BF16)
            to_mate(sub).start()
        mi.wait_recv()
        for sub in range(2):
            to_sibling(sub).wait_recv()
            total[pl.ds(HALF * sub, HALF), :] = fin_r[sub].astype(F32)

    my_gain = gain_row(grp)
    stats = mi_r[...]
    means = jnp.concatenate([to_col(stats[q : q + 1, :]) for q in range(3)], axis=0)
    scales = jnp.concatenate([to_col(stats[q : q + 1, :]) for q in range(3, 6)], axis=0)
    halves = []
    for sub in range(2):
        part_rows = slice(HALF * sub, HALF * (sub + 1))
        iv = scales[part_rows, :]
        normed = own[sub, pl.ds(0, HALF), :].astype(F32) * iv
        ct = own[sub, pl.ds(HALF, HALF), :].astype(F32)
        grad = total[pl.ds(HALF * sub, HALF), :] * my_gain
        halves.append((ct + iv * (grad - normed * means[part_rows, :])).astype(BF16))
    embedded = jnp.concatenate(halves, axis=0)

    for k in range(NP):
        snd[k] = jnp.dot(
            place[pl.ds(CAP * k, CAP), :], embedded, preferred_element_type=F32
        ).astype(BF16)

    def row_copy(k):
        peer = m16(dp + k)
        return remote(snd.at[peer], rows_out.at[dp], rw_ss, rw_rs, (peer, z, c))

    for k in range(1, NP):
        row_copy(k).start()
    own_row_copy = pltpu.make_async_copy(snd.at[dp], rows_out.at[dp], small_sem.at[4])
    own_row_copy.start()

    for b in range(NB):
        ref = w.at[b, pl.ds(0, 3), pl.ds(0, 3)]
        remote(ref, ref, ag_ss.at[b], ag_rs.at[b, 0], sibling).wait_send()
        shared(b).wait_send()
    for hf in range(2):
        ex_mate(hf).wait_send()
        ref = tc.at[hf, pl.ds(0, 7)]
        remote(ref, ref, tk_ss.at[hf], tk_rs.at[hf, 0, 0], sibling).wait_send()

    def ring_sent(kind):
        remote(
            rs_s.at[kind], rs_r.at[kind], rg_ss.at[kind], rg_rs.at[kind, 0, 0], sibling
        ).wait_send()

    ring_sent(0)
    for sub in range(2):
        to_mate(sub).wait_send()
    all_ids.wait_send()

    @pl.when(at_home)
    def _():
        ring_sent(1)
        rm_many(7).wait_send()
        mi.wait_send()

    @pl.when(away)
    def _():
        remote(xs, xr, xf_ss, xf_rs.at[0], sibling).wait_send()
        rm_many(8).wait_send()
        for hf in range(2):
            ex_sib(hf, False).wait_send()
        for b in range(NB):
            half(b, v.at[b, y], False).wait_send()

    all_rows = remote(snd.at[others], rows_out.at[others], rw_ss, rw_rs, sibling)
    ids_done.wait()
    own_row_copy.wait()
    all_rows.wait_recv()
    all_rows.wait_send()


def update_kernel(
    ids_h, rows_h, table, accum, table_out, accum_out, ids, rows, tab, acc, sem, in_sem, out_sem
):
    small = [
        pltpu.make_async_copy(src, dst, sem.at[i])
        for i, (src, dst) in enumerate(((ids_h, ids), (rows_h, rows), (accum, acc)))
    ]
    for copy in small:
        copy.start()

    def block(i):
        return pl.ds(i * STEP, STEP)

    loads = [
        pltpu.make_async_copy(table.at[0, block(i)], tab.at[block(i)], in_sem.at[i])
        for i in range(ROWS // STEP)
    ]
    stores = [
        pltpu.make_async_copy(tab.at[block(i)], table_out.at[0, block(i)], out_sem.at[i])
        for i in range(ROWS // STEP)
    ]
    loads[0].start()
    for copy in small:
        copy.wait()
    for copy in loads[1:]:
        copy.start()
    for i in range(ROWS // STEP):
        row = lax.broadcasted_iota(jnp.int32, (STEP, SLOTS), 0) + i * STEP
        hot = jnp.where(row == ids[0:1, :], 1.0, 0.0).astype(BF16)
        grad = jnp.dot(hot, rows[...], preferred_element_type=F32)
        square = jnp.sum(grad * grad, axis=1, keepdims=True) * (1.0 / FW)
        loads[i].wait()
        for q in range(STEP // 128):
            part = slice(128 * q, 128 * (q + 1))
            here = pl.ds(i * STEP + 128 * q, 128)
            fresh = to_col(acc[0:1, here]) + square[part, :]
            acc[0:1, here] = to_row(fresh)
            tab[here, :] = tab[here, :] - LEARNING_RATE * grad[part, :] * lax.rsqrt(fresh)
        stores[i].start()
    accum_store = pltpu.make_async_copy(acc, accum_out, sem.at[3])
    accum_store.start()
    for copy in stores:
        copy.wait()
    accum_store.wait()


def shards(
    tokens, cotangent, norm_gain, gate_weight, up_weight, down_weight, table, accum, owner, slot_row
):
    any_space = pl.BlockSpec(memory_space=pl.ANY)
    dma = pltpu.SemaphoreType.DMA
    rows, ids = pl.pallas_call(
        main_kernel,
        out_shape=(
            jax.ShapeDtypeStruct((NP, CAP, FW), BF16),
            jax.ShapeDtypeStruct((8, SLOTS), jnp.int32),
        ),
        in_specs=[
            any_space,
            any_space,
            any_space,
            any_space,
            any_space,
            any_space,
            any_space,
            any_space,
        ],
        out_specs=(any_space, any_space),
        scratch_shapes=[
            pltpu.VMEM((1, NC * FW), F32),
            pltpu.VMEM((1, TOK), jnp.int32),
            pltpu.VMEM((1, TOK), jnp.int32),
            pltpu.VMEM((8, SLOTS), jnp.int32),
            pltpu.VMEM((NB, 4, 4, UNIT, FW), BF16),
            pltpu.VMEM((NB, 4, UNIT, FW), BF16),
            pltpu.VMEM((NB, 2, QA // 2, FW), BF16),
            pltpu.VMEM((NB, 2, 4, QB // 2, FW), BF16),
            pltpu.VMEM((2, TOK, FW), BF16),
            pltpu.VMEM((2, 8, 2, TOK, FW), BF16),
            pltpu.VMEM((NC, TOK, FW), BF16),
            pltpu.VMEM((NC, TOK, FW), F32),
            pltpu.VMEM((TOK, 1), F32),
            pltpu.VMEM((TOK, FW), BF16),
            pltpu.VMEM((TOK, HB), F32),
            pltpu.VMEM((8, TOK, FW), BF16),
            pltpu.VMEM((8, TOK, FW), BF16),
            pltpu.VMEM((2, 2, 7, HALF, FW), BF16),
            pltpu.VMEM((2, 2, 7, HALF, FW), BF16),
            pltpu.VMEM((2, HALF, FW), BF16),
            pltpu.VMEM((2, HALF, FW), BF16),
            pltpu.VMEM((TOK, FW), F32),
            pltpu.VMEM((8, 128), F32),
            pltpu.VMEM((16, 8, 128), F32),
            pltpu.VMEM((8, 128), F32),
            pltpu.VMEM((8, 128), F32),
            pltpu.VMEM((SLOTS, TOK), BF16),
            pltpu.VMEM((NP, 8, SLOTS), F32),
            pltpu.VMEM((NP, 8, SLOTS), F32),
            pltpu.VMEM((NP, CAP, FW), BF16),
            dma((5,)),
            dma((NB,)),
            dma((8,)),
            dma((NB,)),
            dma((NB,)),
            pltpu.SemaphoreType.REGULAR((NB,)),
            dma((NB,)),
            dma((NB, 4)),
            dma((NB,)),
            dma((NB,)),
            dma((2, 2)),
            dma((2, 3)),
            dma((2,)),
            dma((2, 4, 2)),
            dma(()),
            dma((8,)),
            dma((2,)),
            dma((2, 2, 7)),
            dma((2,)),
            dma((2,)),
            dma(()),
            dma(()),
            dma(()),
            dma(()),
            dma(()),
            dma(()),
            dma(()),
            dma(()),
        ],
        compiler_params=pltpu.CompilerParams(
            collective_id=0, has_side_effects=True, vmem_limit_bytes=61 * 1024 * 1024
        ),
    )(
        tokens,
        cotangent,
        norm_gain.reshape(1, NC * FW),
        gate_weight,
        up_weight,
        down_weight,
        owner.reshape(1, TOK),
        slot_row.reshape(1, TOK),
    )
    blocks = ROWS // STEP
    return pl.pallas_call(
        update_kernel,
        out_shape=(
            jax.ShapeDtypeStruct(table.shape, F32),
            jax.ShapeDtypeStruct(accum.shape, F32),
        ),
        in_specs=[any_space] * 4,
        out_specs=(any_space, any_space),
        scratch_shapes=[
            pltpu.VMEM((8, SLOTS), jnp.int32),
            pltpu.VMEM((SLOTS, FW), BF16),
            pltpu.VMEM((ROWS, FW), F32),
            pltpu.VMEM((1, ROWS), F32),
            dma((4,)),
            dma((blocks,)),
            dma((blocks,)),
        ],
        compiler_params=pltpu.CompilerParams(vmem_limit_bytes=60 * 1024 * 1024),
    )(ids, rows.reshape(SLOTS, FW), table, accum)


def solution(mesh):
    in_specs = (
        P("dp", ("table", "tensor")),
        P("dp", ("table", "tensor")),
        P(),
        P("dp", ("table", "tensor")),
        P("dp", ("table", "tensor")),
        P(("table", "tensor"), "dp"),
        P(("table", "tensor"), "dp", None),
        P(("table", "tensor"), "dp"),
        P(("table", "tensor"), "dp", None),
        P(("table", "tensor"), "dp", None),
    )
    out_specs = (P(("table", "tensor"), "dp", None), P(("table", "tensor"), "dp"))
    return jax.shard_map(shards, mesh=mesh, in_specs=in_specs, out_specs=out_specs, check_vma=False)
```
